32 devices in a mesh: tm: 8 (over z, x), lat: 4 (over y, core).
Axes of the slice: x: 2, y: 2, z: 4, core: 2. Of those that a mesh axis runs over, the one named last changes fastest.
Arguments:
- states: float32 [8, 3, 32, 2048], P('tm', None, 'lat'), may hold values from -1.5 to 1.5
- background: float32 [3, 32, 2048], P(None, 'lat'), may hold values from -1.5 to 1.5
- error_std: float32 [3, 32, 2048], P(None, 'lat'), may hold values from 0.5 to 2
- land_mask: int32 [8, 128], P('lat'), may hold values 0 or 1
- obs_cells: int32 [8, 512], P('tm', 'lat'), may hold values from 0 to 16383
- measurement_moments: int32 [8, 512], P('tm', 'lat'), may hold values from 0 to 3
- obs_values: float32 [8, 512], P('tm', 'lat'), may hold values from -2.4 to 2.4
- obs_error: float32 [8, 512], P('tm', 'lat'), may hold values from 0.3 to 1
Outputs:
- estimated_openings: float32 [8, 3, 32, 2048], P('tm', None, 'lat')
- slid: float32 [8, 3, 32, 2048], P('tm', None, 'lat')
- costs: float32 [2], replicated
The draws below stay inside these ranges and needn't reach their ends.
Inputs may be any that keep to these rules, and one draw needn't show every extreme that they name: `obs_cells`: cell index within the band: row within the band times 2048 plus column. `land_mask`: each entry covers 4 x 16 cells.
All inputs are finite; a program needn't handle non-finite values. No bound on the sum of `land_mask` on one device may be relied on, other than what follows from the above.
Results may differ from the reference program's by a relative error of at most 0.0003.
Values sent between devices are 32-bit elements; how exact they have to be, the bound alone decides.
A program may use at most 64 MiB of HBM per device.

```python
import math
import jax
import jax.numpy as jnp
from jax import lax

LAT_DEV = 8
NLON = 2048
OBS_DEV = 128
STEPS = 4
ITERS = 2
TILE_LAT = 4
TILE_LON = 16
NT = 8
NLAT = 32
OBS = 512
N_TM = 8
N_LAT = 4


def draw_obs_values(key, part):
    window_rows = jnp.arange(NT, dtype=jnp.float32)[:, None]
    rising = 1.0 + 2.0 * window_rows / max(NT - 1, 1)
    base_values = jnp.clip(jax.random.normal(key, (NT, OBS), jnp.float32), -4.0, 4.0) * 0.2
    return jnp.clip(base_values * rising, -2.4, 2.4)


def touch_ends(array, key, low, high):
    extent = array.shape
    spot = [jax.random.randint(jax.random.fold_in(key, axis), (), 0, extent[axis]) for axis in range(len(extent))]
    array = array.at[tuple(spot)].set(low)
    longest = extent.index(max(extent))
    spot[longest] = (spot[longest] + 1) % extent[longest]
    return array.at[tuple(spot)].set(high)


def level_of(key, dims, split, least, largest):
    level = 1.0
    for position, shards_of in split:
        heights = jax.random.uniform(jax.random.fold_in(jax.random.fold_in(key, 6), position), (shards_of,), jnp.float32, least / len(split), largest / len(split))
        level = level * jnp.repeat(jnp.exp(heights), dims[position] // shards_of).reshape((-1,) + (1,) * (len(dims) - 1 - position))
    return level


def noise(stream_key, extent, scale, reach, shards=(), kind=jnp.bfloat16):
    array = jax.random.normal(stream_key, extent, jnp.float32) * scale
    if len(shards) > 0:
        array = level_of(stream_key, extent, shards, -0.22, 0.18) * array
    return jnp.clip(array, min=-reach, max=reach).astype(kind)


def setup_inputs(seed: int = 0) -> dict:
    splits = jax.random.split(jax.random.key(seed), 9)
    return {
        "states": noise(splits[0], (NT, 3, NLAT, NLON), 0.3, 1.5, ((0, 8), (2, 4)), jnp.float32),
        "background": noise(splits[1], (3, NLAT, NLON), 0.3, 1.5, ((1, 4),), jnp.float32),
        "error_std": jnp.clip(jnp.exp(math.log(2.0) - 1.3862944 * jax.random.uniform(splits[2], (3, NLAT, NLON), jnp.float32) ** level_of(splits[2], (3, NLAT, NLON), ((1, 4),), -0.2, 0.2)), 0.5, 2.0),
        "land_mask": touch_ends((jax.random.randint(splits[3], (NLAT // TILE_LAT, NLON // TILE_LON), 0, 8) < 7).astype(jnp.int32), jax.random.fold_in(splits[3], 1), 0, 1),
        "obs_cells": touch_ends(jax.random.randint(splits[4], (NT, OBS), 0, LAT_DEV * NLON), jax.random.fold_in(splits[4], 1), 0, (LAT_DEV * NLON) - 1).astype(jnp.int32),
        "measurement_moments": touch_ends(jax.random.randint(splits[5], (NT, OBS), 0, STEPS), jax.random.fold_in(splits[5], 1), 0, STEPS - 1).astype(jnp.int32),
        "obs_values": draw_obs_values(jax.random.fold_in(splits[8], 71), 0),
        "obs_error": jnp.clip(jnp.exp(math.log(1.0) - 1.2039728 * jax.random.uniform(splits[7], (NT, OBS), jnp.float32) ** level_of(splits[7], (NT, OBS), ((0, 8), (1, 4)), -0.2, 0.2)), 0.3, 1.0),
    }


TIME_STEP = 0.25
MEAN_DEPTH = 1.0
GRAVITY = 1.0
DRAG_RATE = 0.02
STEP_LENGTH = 0.3
CORIOLIS_MEAN = 0.3
CORIOLIS_SLOPE = 0.2
EPSILON = 1e-06

def expand_mask(land_mask):
    tiles_lat, tiles_lon = land_mask.shape
    grown = jnp.broadcast_to(land_mask[:, None, :, None], (tiles_lat, TILE_LAT, tiles_lon, TILE_LON))
    return grown.reshape(tiles_lat * TILE_LAT, tiles_lon * TILE_LON).astype(jnp.float32)

def zonal_diff(field):
    return 0.5 * (jnp.roll(field, -1, axis=1) - jnp.roll(field, 1, axis=1))

def merid_diff(field):
    return 0.5 * (field[2:] - field[:-2])

def model_step(padded, coriolis, ocean_mask):
    interior = padded[:, 1:-1]
    height, eastward, northward = (interior[0], interior[1], interior[2])
    height_pad, east_pad, north_pad = (padded[0], padded[1], padded[2])
    d_height = -(zonal_diff((MEAN_DEPTH + height) * eastward) + merid_diff((MEAN_DEPTH + height_pad) * north_pad))
    d_east = coriolis * northward - GRAVITY * zonal_diff(height) - eastward * zonal_diff(eastward) - northward * merid_diff(east_pad) - DRAG_RATE * eastward
    d_north = -coriolis * eastward - GRAVITY * merid_diff(height_pad) - eastward * zonal_diff(northward) - northward * merid_diff(north_pad) - DRAG_RATE * northward
    return interior + TIME_STEP * ocean_mask * jnp.stack([d_height, d_east, d_north])

def reference(states, background, error_std, land_mask, obs_cells, measurement_moments, obs_values, obs_error):
    ocean_mask = expand_mask(land_mask)
    total_rows = LAT_DEV * N_LAT
    latitude = jnp.arange(total_rows, dtype=jnp.float32)[:, None]
    coriolis = CORIOLIS_MEAN + CORIOLIS_SLOPE * (latitude / total_rows - 0.5)
    band_index = jnp.arange(OBS_DEV * N_LAT, dtype=jnp.int32) // OBS_DEV
    linear_grid_points = (obs_cells + (band_index * (LAT_DEV * NLON))[None, :]).astype(jnp.int32)
    variance = error_std * error_std
    precision = 1.0 / (obs_error * obs_error)
    cell_count = 3 * total_rows * NLON

    def run(current, cell_ids, obs_times):
        measured_quantities = jnp.zeros(cell_ids.shape, jnp.float32)
        for substep in range(STEPS):
            padded = jnp.pad(current, ((0, 0), (1, 1), (0, 0)))
            values = jnp.take(current[0].reshape(-1), cell_ids)
            measured_quantities = measured_quantities + jnp.where(obs_times == substep, values, 0.0)
            current = model_step(padded, coriolis, ocean_mask)
        return (current, measured_quantities)

    def integrate_segment_parts(members):
        return run(members[0], members[1], members[2])

    def pullback(members):
        current, cell_ids, obs_times, force, obs_force = members
        _, backward = jax.vjp(lambda start: run(start, cell_ids, obs_times), current)
        return backward((force, obs_force))[0]
    estimated_openings = states
    costs = []
    for iteration in range(ITERS):
        predicted_closing_condition, measured_quantities = lax.map(integrate_segment_parts, (estimated_openings, linear_grid_points, measurement_moments))
        prior_interval = jnp.concatenate([jnp.zeros_like(predicted_closing_condition[:1]), predicted_closing_condition[:-1]])
        own_term = jnp.concatenate([(estimated_openings[:1] - background[None]) / variance[None], (estimated_openings[1:] - prior_interval[1:]) / variance[None]])
        end_force = -jnp.concatenate([own_term[1:], jnp.zeros_like(own_term[:1])])
        misfit = measured_quantities - obs_values
        weighted = misfit * precision
        total_cost = 0.5 * (jnp.sum(misfit * weighted) + jnp.sum(own_term * own_term * variance[None]))
        adjoint_start = lax.map(pullback, (estimated_openings, linear_grid_points, measurement_moments, end_force, weighted))
        gradient = own_term + adjoint_start
        direction = variance[None] * gradient
        steepness = jnp.sum(gradient * direction)
        step_scale = STEP_LENGTH / jnp.sqrt(steepness / (N_TM * cell_count) + EPSILON)
        estimated_openings = estimated_openings - step_scale * direction
        costs.append(total_cost / cell_count)
    final_end, _ = lax.map(integrate_segment_parts, (estimated_openings, linear_grid_points, measurement_moments))
    slid = jnp.concatenate([estimated_openings[1:], final_end[-1:]])
    return (estimated_openings, slid, jnp.stack(costs))
```

```python
import functools

import jax
import jax.numpy as jnp
from jax import lax
from jax.experimental import pallas as pl
from jax.experimental.pallas import tpu as pltpu
from jax.sharding import PartitionSpec as P

STEPS = 4
ITERS = 2
TILE_LAT = 4
TILE_LON = 16

TIME_STEP = 0.25
MEAN_DEPTH = 1.0
DRAG_RATE = 0.02
STEP_LENGTH = 0.3
CORIOLIS_MEAN = 0.3
CORIOLIS_SLOPE = 0.2
EPSILON = 1e-06

MESH = pl.DeviceIdType.MESH
LANES = 128
WIDTH = 512
DIRECT_MAX = 64


def split3(x):
    hi = x.astype(jnp.bfloat16)
    rest = x - hi.astype(jnp.float32)
    mid = rest.astype(jnp.bfloat16)
    low = (rest - mid.astype(jnp.float32)).astype(jnp.bfloat16)
    return jnp.concatenate([hi, mid, low], axis=0)


def join3(y):
    n = y.shape[0] // 3
    return (y[2 * n :] + y[n : 2 * n]) + y[:n]


def fold_lanes(x):
    total = x[:, :LANES]
    for c in range(LANES, x.shape[1], LANES):
        total = total + x[:, c : c + LANES]
    return jnp.sum(total, axis=0, keepdims=True)


def kernel(
    n_tm, n_lat,
    states, background, error_std, land_mask, obs_cells, obs_moments, obs_values, obs_error,
    est_out, slid_out, costs_out,
    xs, deriv, lam, forcing, onehot, gain, cor, masks, variance, inv_var,
    xnext, fe_prev, adj_in, dir_buf, dir_halo, dir_next, parts, parts_tm,
    ssem, rsem,
):
    tm = lax.axis_index("tm")
    lat = lax.axis_index("lat")
    rows = background.shape[1]
    lon = background.shape[2]
    wide = 2 * rows
    half = STEPS
    width = min(WIDTH, lon)
    tiles = lon // width
    total_rows = rows * n_lat
    cell_count = 3 * total_rows * lon
    n_dev = n_tm * n_lat
    me = tm * n_lat + lat
    has_up = lat > 0
    has_down = lat < n_lat - 1
    has_prev = tm > 0
    has_next = tm < n_tm - 1
    up = {"lat": lat - 1}
    down = {"lat": lat + 1}
    before = {"tm": tm - 1}
    after = {"tm": tm + 1}
    direct = n_dev <= DIRECT_MAX

    def all_partner(d):
        rank = (me + d) % n_dev
        return {"tm": rank // n_lat, "lat": rank % n_lat}

    def lat_partner(d):
        return {"lat": (lat + d) % n_lat}

    def tm_partner(d):
        return {"tm": (tm + d) % n_tm}

    barrier = pltpu.get_barrier_semaphore()
    if direct:
        partners = [all_partner(d) for d in range(1, n_dev)]
    else:
        partners = [lat_partner(d) for d in range(1, n_lat)]
        partners += [tm_partner(d) for d in range(1, n_tm)]
    for partner in partners:
        pl.semaphore_signal(barrier, inc=1, device_id=partner, device_id_type=MESH)

    def remote(src, dst, k, device):
        return pltpu.make_async_remote_copy(
            src_ref=src, dst_ref=dst, send_sem=ssem.at[k], recv_sem=rsem.at[k],
            device_id=device, device_id_type=MESH,
        )

    pending = []

    def send(cond, src, dst, k, device):
        @pl.when(cond)
        def _():
            remote(src, dst, k, device).start()

        pending.append((cond, src, k, device))

    def drain():
        for cond, src, k, device in pending:
            @pl.when(cond)
            def _(src=src, k=k, device=device):
                remote(src, src, k, device).wait_send()
        pending.clear()

    def arrive(cond, dst, k, device):
        @pl.when(cond)
        def _():
            remote(dst, dst, k, device).wait_recv()

    zeros_half = jnp.zeros((3, half, lon), jnp.float32)
    lo, hi = slice(0, half), slice(half, rows)
    lo_w, hi_w = slice(rows, rows + half), slice(rows + half, wide)
    own = slice(0, rows)

    @pl.when(lat == n_lat - 1)
    def _():
        xs[0, :, lo_w, :] = zeros_half
        masks[lo_w, :] = jnp.zeros((half, LANES), jnp.float32)
        for it in range(ITERS):
            adj_in[it, :, hi, :] = zeros_half
            dir_halo[it, :, lo, :] = zeros_half

    @pl.when(lat == 0)
    def _():
        xs[0, :, hi_w, :] = zeros_half
        masks[hi_w, :] = jnp.zeros((half, LANES), jnp.float32)
        for it in range(ITERS):
            adj_in[it, :, lo, :] = zeros_half
            dir_halo[it, :, hi, :] = zeros_half

    @pl.when(tm == n_tm - 1)
    def _():
        xnext[...] = jnp.zeros(xnext.shape, jnp.float32)
        for it in range(ITERS):
            dir_next[it] = jnp.zeros(xnext.shape, jnp.float32)

    @pl.when(tm == 0)
    def _():
        for it in range(ITERS):
            fe_prev[it] = background[...]

    mask = land_mask[...].astype(jnp.float32)
    tile_cols = mask.shape[1]
    masks[own, :] = jnp.concatenate(
        [jnp.broadcast_to(mask[i : i + 1], (TILE_LAT, tile_cols)) for i in range(rows // TILE_LAT)],
        axis=0,
    )

    pl.semaphore_wait(barrier, len(partners))

    send(has_up, masks.at[lo], masks.at[lo_w], 0, up)
    send(has_down, masks.at[hi], masks.at[hi_w], 1, down)
    send(has_up, states.at[0, :, lo], xs.at[0, :, lo_w], 2, up)
    send(has_down, states.at[0, :, hi], xs.at[0, :, hi_w], 3, down)
    send(has_prev, states.at[0], xnext, 4, before)

    xs[0, :, own, :] = states[0]
    var = error_std[...] * error_std[...]
    variance[...] = var
    inv_var[...] = 1.0 / var
    cells = obs_cells[...]
    n_obs = cells.shape[1]
    cell_row = jnp.zeros_like(cells)
    for r in range(1, rows):
        cell_row = cell_row + (cells >= r * lon).astype(jnp.int32)
    cell_col = cells - cell_row * lon
    onehot[...] = (
        lax.broadcasted_iota(jnp.int32, (lon, n_obs), 0) == cell_col
    ).astype(jnp.float32).astype(jnp.bfloat16)
    taken = (
        lax.broadcasted_iota(jnp.int32, (STEPS * rows, n_obs), 0)
        == obs_moments[...] * rows + cell_row
    ).astype(jnp.float32)
    targets = obs_values[...]
    precision = 1.0 / (obs_error[...] * obs_error[...])
    r_id = lax.broadcasted_iota(jnp.int32, (wide, LANES), 0)
    r_id = jnp.where(r_id < rows + half, r_id, r_id - wide) + lat * rows
    cor[...] = CORIOLIS_MEAN + CORIOLIS_SLOPE * (r_id.astype(jnp.float32) / total_rows - 0.5)
    lam[STEPS, :, rows:wide, :] = jnp.zeros((3, rows, lon), jnp.float32)

    arrive(has_down, masks.at[lo_w], 0, down)
    arrive(has_up, masks.at[hi_w], 1, up)
    first_col = lax.broadcasted_iota(jnp.int32, (tile_cols, lon), 0) * TILE_LON
    col = lax.broadcasted_iota(jnp.int32, (tile_cols, lon), 1)
    grow = ((col >= first_col) & (col < first_col + TILE_LON)).astype(jnp.float32)
    gain[...] = TIME_STEP * jnp.dot(
        masks[...].astype(jnp.bfloat16), grow.astype(jnp.bfloat16),
        preferred_element_type=jnp.float32,
    )
    arrive(has_down, xs.at[0, :, lo_w], 2, down)
    arrive(has_up, xs.at[0, :, hi_w], 3, up)

    def ext(ref, index, j):
        c = j * width
        left = (c - LANES) % lon
        right = (c + width) % lon
        return jnp.concatenate(
            [
                ref[index + (slice(None), slice(left, left + LANES))],
                ref[index + (slice(None), slice(c, c + width))],
                ref[index + (slice(None), slice(right, right + LANES))],
            ],
            axis=-1,
        )

    def mid(e):
        return e[:, LANES : LANES + width]

    def dx2(e):
        return mid(pltpu.roll(e, width + 2 * LANES - 1, 1)) - mid(pltpu.roll(e, 1, 1))

    def east(e):
        return mid(pltpu.roll(e, width + 2 * LANES - 1, 1))

    def west(e):
        return mid(pltpu.roll(e, 1, 1))

    def north(a):
        return pltpu.roll(a, wide - 1, 0)

    def south(a):
        return pltpu.roll(a, 1, 0)

    def dy2(a):
        return north(a) - south(a)

    def coriolis():
        return jnp.concatenate([cor[...]] * (width // LANES), axis=-1)

    def forward_step(s, carry):
        for j in range(tiles):
            span = slice(j * width, (j + 1) * width)
            he, ue, ve = (ext(xs, (s, f), j) for f in range(3))
            h, u, v = mid(he), mid(ue), mid(ve)
            h_e, h_w, u_e, u_w = east(he), west(he), east(ue), west(ue)
            h_n, h_s, v_n, v_s = north(h), south(h), north(v), south(v)
            ux = 0.5 * (u_e - u_w)
            vx = 0.5 * dx2(ve)
            uy = 0.5 * dy2(u)
            vy = 0.5 * (v_n - v_s)
            g = gain[:, span]
            f = coriolis()
            dh = -0.5 * (
                ((MEAN_DEPTH + h_e) * u_e - (MEAN_DEPTH + h_w) * u_w)
                + ((MEAN_DEPTH + h_n) * v_n - (MEAN_DEPTH + h_s) * v_s)
            )
            du = f * v - 0.5 * (h_e - h_w) - u * ux - v * uy - DRAG_RATE * u
            dv = -f * u - 0.5 * (h_n - h_s) - u * vx - v * vy - DRAG_RATE * v
            xs[s + 1, 0, :, span] = h + g * dh
            xs[s + 1, 1, :, span] = u + g * du
            xs[s + 1, 2, :, span] = v + g * dv
            deriv[s, 0, :, span] = ux
            deriv[s, 1, :, span] = uy
            deriv[s, 2, :, span] = vx
            deriv[s, 3, :, span] = vy
        return carry

    def adjoint_step(i, carry):
        s = STEPS - 1 - i
        for j in range(tiles):
            span = slice(j * width, (j + 1) * width)
            ge = ext(gain, (), j)
            lh, lu, lv = (ext(lam, (s + 1, f), j) for f in range(3))
            ae, be, ce = lh * ge, lu * ge, lv * ge
            ue = ext(xs, (s, 1), j)
            a, b, c, u = mid(ae), mid(be), mid(ce), mid(ue)
            v = xs[s, 2, :, span]
            depth = 0.5 * (MEAN_DEPTH + xs[s, 0, :, span])
            f = coriolis()
            ax, ay = dx2(ae), dy2(a)
            obs = jnp.concatenate(
                [forcing[s, :, span], jnp.zeros((rows, width), jnp.float32)], axis=0
            )
            lam[s, 0, :, span] = (
                mid(lh) + obs + 0.5 * (u * ax + v * ay + dx2(be) + dy2(c))
            )
            lam[s, 1, :, span] = (
                mid(lu)
                + depth * ax
                + 0.5 * (dx2(ue * be) + dy2(v * b))
                - b * (deriv[s, 0, :, span] + DRAG_RATE)
                - c * (f + deriv[s, 2, :, span])
            )
            lam[s, 2, :, span] = (
                mid(lv)
                + depth * ay
                + 0.5 * (dx2(ue * ce) + dy2(v * c))
                + b * (f - deriv[s, 1, :, span])
                - c * (deriv[s, 3, :, span] + DRAG_RATE)
            )
        return carry

    def exchange(buf, value, k, size, mine, partner):
        buf[mine] = value
        for d in range(1, size):
            remote(buf.at[mine], buf.at[mine], k, partner(d)).start()

    def collect(buf, k, size, partner):
        remote(buf.at[0 : size - 1], buf.at[0 : size - 1], k, partner(1)).wait_recv()
        total = jnp.sum(buf[...], axis=0)
        return total

    def sent(buf, k, size, partner):
        remote(buf.at[0 : size - 1], buf.at[0 : size - 1], k, partner(1)).wait_send()

    scale = None
    for it in range(ITERS):
        base = 5 + 8 * it
        lax.fori_loop(0, STEPS, forward_step, 0)
        send(has_next, xs.at[STEPS, :, own], fe_prev.at[it], base, after)

        heights = jnp.concatenate([xs[s, 0, own, :] for s in range(STEPS)], axis=0)
        seen = join3(
            jnp.dot(split3(heights), onehot[...], preferred_element_type=jnp.float32)
        )
        misfit = jnp.sum(seen * taken, axis=0, keepdims=True) - targets
        weighted = misfit * precision
        spread = join3(
            lax.dot_general(
                split3(taken * weighted), onehot[...], (((1,), (1,)), ((), ())),
                preferred_element_type=jnp.float32,
            )
        )
        for s in range(STEPS):
            forcing[s] = spread[s * rows : (s + 1) * rows]

        if it == 0:
            arrive(has_next, xnext, 4, after)
        else:
            arrive(has_next, dir_next.at[it - 1], base - 8 + 5, after)
            xnext[...] = xnext[...] - scale * dir_next[it - 1]

        @pl.when(has_next)
        def _():
            lam[STEPS, :, own, :] = (xs[STEPS, :, own, :] - xnext[...]) * inv_var[...]

        @pl.when(tm == n_tm - 1)
        def _():
            lam[STEPS, :, own, :] = jnp.zeros((3, rows, lon), jnp.float32)

        lax.fori_loop(0, STEPS, adjoint_step, 0)
        send(has_down, lam.at[0, :, lo_w], adj_in.at[it, :, lo], base + 1, down)
        send(has_up, lam.at[0, :, hi_w], adj_in.at[it, :, hi], base + 2, up)

        arrive(has_prev, fe_prev.at[it], base, before)
        cost = misfit * weighted
        for f in range(3):
            gap = xs[0, f, own, :] - fe_prev[it, f]
            cost = cost + fold_lanes(gap * gap * inv_var[f])
            dir_buf[it, f] = gap + variance[f] * lam[0, f, own, :]
        arrive(has_up, adj_in.at[it, :, lo], base + 1, up)
        arrive(has_down, adj_in.at[it, :, hi], base + 2, down)
        steep = jnp.zeros((1, LANES), jnp.float32)
        for f in range(3):
            direction = dir_buf[it, f] + variance[f] * adj_in[it, f]
            dir_buf[it, f] = direction
            steep = steep + fold_lanes(direction * direction * inv_var[f])

        message = jnp.concatenate([steep, cost], axis=0)
        if direct:
            exchange(parts.at[it], message, base + 6, n_dev, me, all_partner)
        else:
            exchange(parts.at[it], message, base + 6, n_lat, lat, lat_partner)
        send(has_up, dir_buf.at[it, :, lo], dir_halo.at[it, :, lo], base + 3, up)
        send(has_down, dir_buf.at[it, :, hi], dir_halo.at[it, :, hi], base + 4, down)
        if direct:
            send(has_prev, dir_buf.at[it], dir_next.at[it], base + 5, before)
            total = collect(parts.at[it], base + 6, n_dev, all_partner)
        else:
            total = collect(parts.at[it], base + 6, n_lat, lat_partner)
            exchange(parts_tm.at[it], total, base + 7, n_tm, tm, tm_partner)
            send(has_prev, dir_buf.at[it], dir_next.at[it], base + 5, before)
            total = collect(parts_tm.at[it], base + 7, n_tm, tm_partner)
        steepness = jnp.sum(total[0:1], axis=1, keepdims=True)
        scale = STEP_LENGTH / jnp.sqrt(steepness / (n_tm * cell_count) + EPSILON)
        costs_out[it] = jnp.sum(total[1:2]) * (0.5 / cell_count)

        for f in range(3):
            xs[0, f, own, :] = xs[0, f, own, :] - scale * dir_buf[it, f]
        arrive(has_down, dir_halo.at[it, :, lo], base + 3, down)
        arrive(has_up, dir_halo.at[it, :, hi], base + 4, up)
        for f in range(3):
            xs[0, f, rows:wide, :] = xs[0, f, rows:wide, :] - scale * dir_halo[it, f]
        drain()
        if direct:
            sent(parts.at[it], base + 6, n_dev, all_partner)
        else:
            sent(parts.at[it], base + 6, n_lat, lat_partner)
            sent(parts_tm.at[it], base + 7, n_tm, tm_partner)

    est_out[0] = xs[0, :, own, :]
    lax.fori_loop(0, STEPS, forward_step, 0)
    arrive(has_next, dir_next.at[ITERS - 1], 5 + 8 * (ITERS - 1) + 5, after)

    @pl.when(has_next)
    def _():
        slid_out[0] = xnext[...] - scale * dir_next[ITERS - 1]

    @pl.when(tm == n_tm - 1)
    def _():
        slid_out[0] = xs[STEPS, :, own, :]


def shards(n_tm, n_lat, *args):
    states, background = args[0], args[1]
    _, rows, lon = background.shape
    n_obs = args[4].shape[1]
    wide = 2 * rows
    f32 = jnp.float32
    direct = n_tm * n_lat <= DIRECT_MAX
    field = (3, rows, lon)
    sems = 5 + 8 * ITERS
    return pl.pallas_call(
        functools.partial(kernel, n_tm, n_lat),
        out_shape=(
            jax.ShapeDtypeStruct(states.shape, f32),
            jax.ShapeDtypeStruct(states.shape, f32),
            jax.ShapeDtypeStruct((ITERS,), f32),
        ),
        in_specs=[pl.BlockSpec(memory_space=pltpu.VMEM)] * 8,
        out_specs=(
            pl.BlockSpec(memory_space=pltpu.VMEM),
            pl.BlockSpec(memory_space=pltpu.VMEM),
            pl.BlockSpec(memory_space=pltpu.SMEM),
        ),
        scratch_shapes=[
            pltpu.VMEM((STEPS + 1, 3, wide, lon), f32),
            pltpu.VMEM((STEPS, 4, wide, lon), f32),
            pltpu.VMEM((STEPS + 1, 3, wide, lon), f32),
            pltpu.VMEM((STEPS, rows, lon), f32),
            pltpu.VMEM((lon, n_obs), jnp.bfloat16),
            pltpu.VMEM((wide, lon), f32),
            pltpu.VMEM((wide, LANES), f32),
            pltpu.VMEM((wide, LANES), f32),
            pltpu.VMEM(field, f32),
            pltpu.VMEM(field, f32),
            pltpu.VMEM(field, f32),
            pltpu.VMEM((ITERS,) + field, f32),
            pltpu.VMEM((ITERS,) + field, f32),
            pltpu.VMEM((ITERS,) + field, f32),
            pltpu.VMEM((ITERS,) + field, f32),
            pltpu.VMEM((ITERS,) + field, f32),
            pltpu.VMEM((ITERS, n_tm * n_lat if direct else n_lat, 2, LANES), f32),
            pltpu.VMEM((ITERS, n_tm, 2, LANES), f32),
            pltpu.SemaphoreType.DMA((sems,)),
            pltpu.SemaphoreType.DMA((sems,)),
        ],
        compiler_params=pltpu.CompilerParams(
            collective_id=0, has_side_effects=True, vmem_limit_bytes=40 * 1024 * 1024
        ),
    )(*args)


def solution(mesh):
    placed = (
        P("tm", None, "lat", None),
        P(None, "lat", None),
        P(None, "lat", None),
        P("lat", None),
        P("tm", "lat"),
        P("tm", "lat"),
        P("tm", "lat"),
        P("tm", "lat"),
    )
    return jax.shard_map(
        functools.partial(shards, mesh.shape["tm"], mesh.shape["lat"]),
        mesh=mesh,
        in_specs=placed,
        out_specs=(P("tm", None, "lat", None), P("tm", None, "lat", None), P()),
        check_vma=False,
    )
```

```python
import functools

import jax
import jax.numpy as jnp
from jax import lax
from jax.experimental import pallas as pl
from jax.experimental.pallas import tpu as pltpu
from jax.sharding import PartitionSpec as P

STEPS = 4
ITERS = 2
TILE_LAT = 4
TILE_LON = 16

TIME_STEP = 0.25
MEAN_DEPTH = 1.0
DRAG_RATE = 0.02
STEP_LENGTH = 0.3
CORIOLIS_MEAN = 0.3
CORIOLIS_SLOPE = 0.2
EPSILON = 1e-06

MESH = pl.DeviceIdType.MESH
LANES = 128
WIDTH = 512
DIRECT_MAX = 64


def split3(x):
    hi = x.astype(jnp.bfloat16)
    rest = x - hi.astype(jnp.float32)
    mid = rest.astype(jnp.bfloat16)
    low = (rest - mid.astype(jnp.float32)).astype(jnp.bfloat16)
    return jnp.concatenate([hi, mid, low], axis=0)


def join3(y):
    n = y.shape[0] // 3
    return (y[2 * n :] + y[n : 2 * n]) + y[:n]


def fold_lanes(x):
    total = x[:, :LANES]
    for c in range(LANES, x.shape[1], LANES):
        total = total + x[:, c : c + LANES]
    return jnp.sum(total, axis=0, keepdims=True)


def kernel(
    n_tm, n_lat,
    states_hbm, background_hbm, error_hbm, mask_hbm, cells_hbm, moments_hbm, values_hbm, obs_err_hbm,
    est_out, slid_out, costs_out,
    xs, deriv, lam, forcing, onehot, gain, cor, masks, variance, inv_var,
    xnext, fe_prev, adj_in, dir_buf, dir_halo, dir_next, parts, parts_tm,
    error_std, land_mask, obs_cells, obs_moments, obs_values, obs_error,
    ssem, rsem, lsem,
):
    tm = lax.axis_index("tm")
    lat = lax.axis_index("lat")
    rows = variance.shape[1]
    lon = variance.shape[2]
    wide = 2 * rows
    half = STEPS
    width = min(WIDTH, lon)
    tiles = lon // width
    total_rows = rows * n_lat
    cell_count = 3 * total_rows * lon
    n_dev = n_tm * n_lat
    me = tm * n_lat + lat
    has_up = lat > 0
    has_down = lat < n_lat - 1
    has_prev = tm > 0
    has_next = tm < n_tm - 1
    up = {"lat": lat - 1}
    down = {"lat": lat + 1}
    before = {"tm": tm - 1}
    after = {"tm": tm + 1}
    direct = n_dev <= DIRECT_MAX

    def wrapped(i, n):
        return jnp.where(i >= n, i - n, i)

    lats = [lat] + [wrapped(lat + d, n_lat) for d in range(1, n_lat)]
    tms = [tm] + [wrapped(tm + d, n_tm) for d in range(1, n_tm)]
    lat_partners = [{"lat": lats[d]} for d in range(1, n_lat)]
    tm_partners = [{"tm": tms[d]} for d in range(1, n_tm)]
    if direct:
        all_partners = [
            {"tm": tms[t], "lat": lats[d]}
            for t in range(n_tm) for d in range(n_lat) if t or d
        ]
        partners = all_partners
    else:
        partners = lat_partners + tm_partners
    barrier = pltpu.get_barrier_semaphore()
    for partner in partners:
        pl.semaphore_signal(barrier, inc=1, device_id=partner, device_id_type=MESH)

    own = slice(0, rows)
    loads = []

    def load(src, dst):
        copy = pltpu.make_async_copy(src, dst, lsem.at[len(loads)])
        copy.start()
        loads.append(copy)

    load(states_hbm.at[0], xs.at[0, :, own])
    load(mask_hbm, land_mask)
    load(error_hbm, error_std)
    load(cells_hbm, obs_cells)
    load(moments_hbm, obs_moments)
    load(values_hbm, obs_values)
    load(obs_err_hbm, obs_error)
    for it in range(ITERS):
        @pl.when(tm == 0)
        def _(it=it):
            pltpu.make_async_copy(background_hbm, fe_prev.at[it], lsem.at[7 + it]).start()

    def remote(src, dst, k, device):
        return pltpu.make_async_remote_copy(
            src_ref=src, dst_ref=dst, send_sem=ssem.at[k], recv_sem=rsem.at[k],
            device_id=device, device_id_type=MESH,
        )

    pending = []
    late = []

    def send(cond, src, dst, k, device, queue=pending):
        @pl.when(cond)
        def _():
            remote(src, dst, k, device).start()

        queue.append((cond, src, k, device))

    def drain(queue):
        for cond, src, k, device in queue:
            @pl.when(cond)
            def _(src=src, k=k, device=device):
                remote(src, src, k, device).wait_send()
        queue.clear()

    def arrive(cond, dst, k, device):
        @pl.when(cond)
        def _():
            remote(dst, dst, k, device).wait_recv()

    zeros_half = jnp.zeros((3, half, lon), jnp.float32)
    lo, hi = slice(0, half), slice(half, rows)
    lo_w, hi_w = slice(rows, rows + half), slice(rows + half, wide)

    @pl.when(lat == n_lat - 1)
    def _():
        xs[0, :, lo_w, :] = zeros_half
        masks[lo_w, :] = jnp.zeros((half, LANES), jnp.float32)
        for it in range(ITERS):
            adj_in[it, :, hi, :] = zeros_half
            dir_halo[it, :, lo, :] = zeros_half

    @pl.when(lat == 0)
    def _():
        xs[0, :, hi_w, :] = zeros_half
        masks[hi_w, :] = jnp.zeros((half, LANES), jnp.float32)
        for it in range(ITERS):
            adj_in[it, :, lo, :] = zeros_half
            dir_halo[it, :, hi, :] = zeros_half

    @pl.when(tm == n_tm - 1)
    def _():
        xnext[...] = jnp.zeros(xnext.shape, jnp.float32)
        for it in range(ITERS):
            dir_next[it] = jnp.zeros(xnext.shape, jnp.float32)

    loads[1].wait()
    mask = land_mask[...].astype(jnp.float32)
    tile_cols = mask.shape[1]
    masks[own, :] = jnp.concatenate(
        [jnp.broadcast_to(mask[i : i + 1], (TILE_LAT, tile_cols)) for i in range(rows // TILE_LAT)],
        axis=0,
    )

    loads[0].wait()
    pl.semaphore_wait(barrier, len(partners))

    send(has_up, masks.at[lo], masks.at[lo_w], 0, up)
    send(has_down, masks.at[hi], masks.at[hi_w], 1, down)
    send(has_up, xs.at[0, :, lo], xs.at[0, :, lo_w], 2, up)
    send(has_down, xs.at[0, :, hi], xs.at[0, :, hi_w], 3, down)
    send(has_prev, xs.at[0, :, own], xnext, 4, before)

    for copy in loads[2:]:
        copy.wait()
    var = error_std[...] * error_std[...]
    variance[...] = var
    inv_var[...] = 1.0 / var
    cells = obs_cells[...]
    n_obs = cells.shape[1]
    cell_row = jnp.zeros_like(cells)
    for r in range(1, rows):
        cell_row = cell_row + (cells >= r * lon).astype(jnp.int32)
    cell_col = cells - cell_row * lon
    onehot[...] = (
        lax.broadcasted_iota(jnp.int32, (lon, n_obs), 0) == cell_col
    ).astype(jnp.float32).astype(jnp.bfloat16)
    taken = (
        lax.broadcasted_iota(jnp.int32, (STEPS * rows, n_obs), 0)
        == obs_moments[...] * rows + cell_row
    ).astype(jnp.float32)
    targets = obs_values[...]
    precision = 1.0 / (obs_error[...] * obs_error[...])
    r_id = lax.broadcasted_iota(jnp.int32, (wide, LANES), 0)
    r_id = jnp.where(r_id < rows + half, r_id, r_id - wide) + lat * rows
    cor[...] = CORIOLIS_MEAN + CORIOLIS_SLOPE * (r_id.astype(jnp.float32) / total_rows - 0.5)
    lam[STEPS, :, rows:wide, :] = jnp.zeros((3, rows, lon), jnp.float32)

    arrive(has_down, masks.at[lo_w], 0, down)
    arrive(has_up, masks.at[hi_w], 1, up)
    first_col = lax.broadcasted_iota(jnp.int32, (tile_cols, lon), 0) * TILE_LON
    col = lax.broadcasted_iota(jnp.int32, (tile_cols, lon), 1)
    grow = ((col >= first_col) & (col < first_col + TILE_LON)).astype(jnp.float32)
    gain[...] = TIME_STEP * jnp.dot(
        masks[...].astype(jnp.bfloat16), grow.astype(jnp.bfloat16),
        preferred_element_type=jnp.float32,
    )
    arrive(has_down, xs.at[0, :, lo_w], 2, down)
    arrive(has_up, xs.at[0, :, hi_w], 3, up)

    def ext(ref, index, j):
        c = j * width
        left = (c - LANES) % lon
        right = (c + width) % lon
        return jnp.concatenate(
            [
                ref[index + (slice(None), slice(left, left + LANES))],
                ref[index + (slice(None), slice(c, c + width))],
                ref[index + (slice(None), slice(right, right + LANES))],
            ],
            axis=-1,
        )

    def mid(e):
        return e[:, LANES : LANES + width]

    def dx2(e):
        return mid(pltpu.roll(e, width + 2 * LANES - 1, 1)) - mid(pltpu.roll(e, 1, 1))

    def east(e):
        return mid(pltpu.roll(e, width + 2 * LANES - 1, 1))

    def west(e):
        return mid(pltpu.roll(e, 1, 1))

    def north(a):
        return pltpu.roll(a, wide - 1, 0)

    def south(a):
        return pltpu.roll(a, 1, 0)

    def dy2(a):
        return north(a) - south(a)

    def coriolis():
        return jnp.concatenate([cor[...]] * (width // LANES), axis=-1)

    def forward_step(s, carry):
        for j in range(tiles):
            span = slice(j * width, (j + 1) * width)
            he, ue, ve = (ext(xs, (s, f), j) for f in range(3))
            h, u, v = mid(he), mid(ue), mid(ve)
            h_e, h_w, u_e, u_w = east(he), west(he), east(ue), west(ue)
            h_n, h_s, v_n, v_s = north(h), south(h), north(v), south(v)
            ux = 0.5 * (u_e - u_w)
            vx = 0.5 * dx2(ve)
            uy = 0.5 * dy2(u)
            vy = 0.5 * (v_n - v_s)
            g = gain[:, span]
            f = coriolis()
            dh = -0.5 * (
                ((MEAN_DEPTH + h_e) * u_e - (MEAN_DEPTH + h_w) * u_w)
                + ((MEAN_DEPTH + h_n) * v_n - (MEAN_DEPTH + h_s) * v_s)
            )
            du = f * v - 0.5 * (h_e - h_w) - u * ux - v * uy - DRAG_RATE * u
            dv = -f * u - 0.5 * (h_n - h_s) - u * vx - v * vy - DRAG_RATE * v
            xs[s + 1, 0, :, span] = h + g * dh
            xs[s + 1, 1, :, span] = u + g * du
            xs[s + 1, 2, :, span] = v + g * dv
            deriv[s, 0, :, span] = ux
            deriv[s, 1, :, span] = uy
            deriv[s, 2, :, span] = vx
            deriv[s, 3, :, span] = vy
        return carry

    def adjoint_step(i, carry):
        s = STEPS - 1 - i
        for j in range(tiles):
            span = slice(j * width, (j + 1) * width)
            ge = ext(gain, (), j)
            lh, lu, lv = (ext(lam, (s + 1, f), j) for f in range(3))
            ae, be, ce = lh * ge, lu * ge, lv * ge
            ue = ext(xs, (s, 1), j)
            a, b, c, u = mid(ae), mid(be), mid(ce), mid(ue)
            v = xs[s, 2, :, span]
            depth = 0.5 * (MEAN_DEPTH + xs[s, 0, :, span])
            f = coriolis()
            ax, ay = dx2(ae), dy2(a)
            obs = jnp.concatenate(
                [forcing[s, :, span], jnp.zeros((rows, width), jnp.float32)], axis=0
            )
            lam[s, 0, :, span] = (
                mid(lh) + obs + 0.5 * (u * ax + v * ay + dx2(be) + dy2(c))
            )
            lam[s, 1, :, span] = (
                mid(lu)
                + depth * ax
                + 0.5 * (dx2(ue * be) + dy2(v * b))
                - b * (deriv[s, 0, :, span] + DRAG_RATE)
                - c * (f + deriv[s, 2, :, span])
            )
            lam[s, 2, :, span] = (
                mid(lv)
                + depth * ay
                + 0.5 * (dx2(ue * ce) + dy2(v * c))
                + b * (f - deriv[s, 1, :, span])
                - c * (deriv[s, 3, :, span] + DRAG_RATE)
            )
        return carry

    def exchange(buf, value, k, size, mine, partner):
        buf[mine] = value
        for device in partner:
            remote(buf.at[mine], buf.at[mine], k, device).start()

    def collect(buf, k, size, partner):
        remote(buf.at[0 : size - 1], buf.at[0 : size - 1], k, partner[0]).wait_recv()
        total = jnp.sum(buf[...], axis=0)
        return total

    def sent(buf, k, size, partner):
        remote(buf.at[0 : size - 1], buf.at[0 : size - 1], k, partner[0]).wait_send()

    scale = None
    for it in range(ITERS):
        base = 5 + 8 * it
        lax.fori_loop(0, STEPS, forward_step, 0)
        send(has_next, xs.at[STEPS, :, own], fe_prev.at[it], base, after)

        heights = jnp.concatenate([xs[s, 0, own, :] for s in range(STEPS)], axis=0)
        seen = join3(
            jnp.dot(split3(heights), onehot[...], preferred_element_type=jnp.float32)
        )
        misfit = jnp.sum(seen * taken, axis=0, keepdims=True) - targets
        weighted = misfit * precision
        spread = join3(
            lax.dot_general(
                split3(taken * weighted), onehot[...], (((1,), (1,)), ((), ())),
                preferred_element_type=jnp.float32,
            )
        )
        for s in range(STEPS):
            forcing[s] = spread[s * rows : (s + 1) * rows]

        if it == 0:
            arrive(has_next, xnext, 4, after)
        else:
            arrive(has_next, dir_next.at[it - 1], base - 8 + 5, after)
            xnext[...] = xnext[...] - scale * dir_next[it - 1]

        @pl.when(has_next)
        def _():
            lam[STEPS, :, own, :] = (xs[STEPS, :, own, :] - xnext[...]) * inv_var[...]

        @pl.when(tm == n_tm - 1)
        def _():
            lam[STEPS, :, own, :] = jnp.zeros((3, rows, lon), jnp.float32)

        lax.fori_loop(0, STEPS, adjoint_step, 0)
        send(has_down, lam.at[0, :, lo_w], adj_in.at[it, :, lo], base + 1, down)
        send(has_up, lam.at[0, :, hi_w], adj_in.at[it, :, hi], base + 2, up)

        arrive(has_prev, fe_prev.at[it], base, before)

        @pl.when(tm == 0)
        def _():
            pltpu.make_async_copy(background_hbm, fe_prev.at[it], lsem.at[7 + it]).wait()

        cost = misfit * weighted
        for f in range(3):
            gap = xs[0, f, own, :] - fe_prev[it, f]
            cost = cost + fold_lanes(gap * gap * inv_var[f])
            dir_buf[it, f] = gap + variance[f] * lam[0, f, own, :]
        arrive(has_up, adj_in.at[it, :, lo], base + 1, up)
        arrive(has_down, adj_in.at[it, :, hi], base + 2, down)
        steep = jnp.zeros((1, LANES), jnp.float32)
        for f in range(3):
            direction = dir_buf[it, f] + variance[f] * adj_in[it, f]
            dir_buf[it, f] = direction
            steep = steep + fold_lanes(direction * direction * inv_var[f])

        message = jnp.concatenate([steep, cost], axis=0)
        if direct:
            exchange(parts.at[it], message, base + 6, n_dev, me, all_partners)
        else:
            exchange(parts.at[it], message, base + 6, n_lat, lat, lat_partners)
        send(has_up, dir_buf.at[it, :, lo], dir_halo.at[it, :, lo], base + 3, up, late)
        send(has_down, dir_buf.at[it, :, hi], dir_halo.at[it, :, hi], base + 4, down, late)
        drain(pending)
        if direct:
            send(has_prev, dir_buf.at[it], dir_next.at[it], base + 5, before, late)
            total = collect(parts.at[it], base + 6, n_dev, all_partners)
        else:
            total = collect(parts.at[it], base + 6, n_lat, lat_partners)
            exchange(parts_tm.at[it], total, base + 7, n_tm, tm, tm_partners)
            send(has_prev, dir_buf.at[it], dir_next.at[it], base + 5, before, late)
            total = collect(parts_tm.at[it], base + 7, n_tm, tm_partners)
        steepness = jnp.sum(total[0:1], axis=1, keepdims=True)
        scale = STEP_LENGTH / jnp.sqrt(steepness / (n_tm * cell_count) + EPSILON)
        costs_out[it] = jnp.sum(total[1:2]) * (0.5 / cell_count)

        for f in range(3):
            xs[0, f, own, :] = xs[0, f, own, :] - scale * dir_buf[it, f]
        arrive(has_down, dir_halo.at[it, :, lo], base + 3, down)
        arrive(has_up, dir_halo.at[it, :, hi], base + 4, up)
        for f in range(3):
            xs[0, f, rows:wide, :] = xs[0, f, rows:wide, :] - scale * dir_halo[it, f]

    est_copy = pltpu.make_async_copy(
        xs.at[0, :, own], est_out.at[0], lsem.at[7 + ITERS]
    )
    est_copy.start()
    lax.fori_loop(0, STEPS, forward_step, 0)
    arrive(has_next, dir_next.at[ITERS - 1], 5 + 8 * (ITERS - 1) + 5, after)

    @pl.when(has_next)
    def _():
        xnext[...] = xnext[...] - scale * dir_next[ITERS - 1]

    @pl.when(tm == n_tm - 1)
    def _():
        xnext[...] = xs[STEPS, :, own, :]

    slid_copy = pltpu.make_async_copy(xnext, slid_out.at[0], lsem.at[8 + ITERS])
    slid_copy.start()
    est_copy.wait()
    slid_copy.wait()
    drain(late)
    for it in range(ITERS):
        base = 5 + 8 * it
        if direct:
            sent(parts.at[it], base + 6, n_dev, all_partners)
        else:
            sent(parts.at[it], base + 6, n_lat, lat_partners)
            sent(parts_tm.at[it], base + 7, n_tm, tm_partners)


def write_out(est, slid, costs, est_out, slid_out, costs_out, est_v, slid_v, costs_s, sem):
    moves = []
    for i, (src, held) in enumerate(((est, est_v), (slid, slid_v), (costs, costs_s))):
        moves.append(pltpu.make_async_copy(src, held, sem.at[i]))
        moves[-1].start()
    outs = []
    for i, (held, dst) in enumerate(((est_v, est_out), (slid_v, slid_out), (costs_s, costs_out))):
        moves[i].wait()
        outs.append(pltpu.make_async_copy(held, dst, sem.at[3 + i]))
        outs[-1].start()
    for copy in outs:
        copy.wait()


def shards(n_tm, n_lat, *args):
    states, background = args[0], args[1]
    _, rows, lon = background.shape
    n_obs = args[4].shape[1]
    wide = 2 * rows
    f32 = jnp.float32
    direct = n_tm * n_lat <= DIRECT_MAX
    field = (3, rows, lon)
    sems = 5 + 8 * ITERS
    est, slid, costs = pl.pallas_call(
        functools.partial(kernel, n_tm, n_lat),
        out_shape=(
            jax.ShapeDtypeStruct(states.shape, f32),
            jax.ShapeDtypeStruct(states.shape, f32),
            jax.ShapeDtypeStruct((ITERS,), f32),
        ),
        in_specs=[pl.BlockSpec(memory_space=pltpu.HBM)] * 8,
        out_specs=(
            pl.BlockSpec(memory_space=pltpu.HBM),
            pl.BlockSpec(memory_space=pltpu.HBM),
            pl.BlockSpec(memory_space=pltpu.SMEM),
        ),
        scratch_shapes=[
            pltpu.VMEM((STEPS + 1, 3, wide, lon), f32),
            pltpu.VMEM((STEPS, 4, wide, lon), f32),
            pltpu.VMEM((STEPS + 1, 3, wide, lon), f32),
            pltpu.VMEM((STEPS, rows, lon), f32),
            pltpu.VMEM((lon, n_obs), jnp.bfloat16),
            pltpu.VMEM((wide, lon), f32),
            pltpu.VMEM((wide, LANES), f32),
            pltpu.VMEM((wide, LANES), f32),
            pltpu.VMEM(field, f32),
            pltpu.VMEM(field, f32),
            pltpu.VMEM(field, f32),
            pltpu.VMEM((ITERS,) + field, f32),
            pltpu.VMEM((ITERS,) + field, f32),
            pltpu.VMEM((ITERS,) + field, f32),
            pltpu.VMEM((ITERS,) + field, f32),
            pltpu.VMEM((ITERS,) + field, f32),
            pltpu.VMEM((ITERS, n_tm * n_lat if direct else n_lat, 2, LANES), f32),
            pltpu.VMEM((ITERS, n_tm, 2, LANES), f32),
            pltpu.VMEM(field, f32),
            pltpu.VMEM(args[3].shape, jnp.int32),
            pltpu.VMEM((1, n_obs), jnp.int32),
            pltpu.VMEM((1, n_obs), jnp.int32),
            pltpu.VMEM((1, n_obs), f32),
            pltpu.VMEM((1, n_obs), f32),
            pltpu.SemaphoreType.DMA((sems,)),
            pltpu.SemaphoreType.DMA((sems,)),
            pltpu.SemaphoreType.DMA((9 + ITERS,)),
        ],
        compiler_params=pltpu.CompilerParams(
            collective_id=0, has_side_effects=True
        ),
    )(*args)
    return pl.pallas_call(
        write_out,
        out_shape=(
            jax.ShapeDtypeStruct(states.shape, f32),
            jax.ShapeDtypeStruct(states.shape, f32),
            jax.ShapeDtypeStruct((ITERS,), f32),
        ),
        in_specs=[pl.BlockSpec(memory_space=pltpu.HBM)] * 3,
        out_specs=(pl.BlockSpec(memory_space=pltpu.HBM),) * 3,
        scratch_shapes=[
            pltpu.VMEM(states.shape, f32),
            pltpu.VMEM(states.shape, f32),
            pltpu.SMEM((ITERS,), f32),
            pltpu.SemaphoreType.DMA((6,)),
        ],
    )(est, slid, costs)


def solution(mesh):
    placed = (
        P("tm", None, "lat", None),
        P(None, "lat", None),
        P(None, "lat", None),
        P("lat", None),
        P("tm", "lat"),
        P("tm", "lat"),
        P("tm", "lat"),
        P("tm", "lat"),
    )
    return jax.shard_map(
        functools.partial(shards, mesh.shape["tm"], mesh.shape["lat"]),
        mesh=mesh,
        in_specs=placed,
        out_specs=(P("tm", None, "lat", None), P("tm", None, "lat", None), P()),
        check_vma=False,
    )
```

```python
import functools

import jax
import jax.numpy as jnp
from jax import lax
from jax.experimental import pallas as pl
from jax.experimental.pallas import tpu as pltpu
from jax.sharding import PartitionSpec as P

STEPS = 4
ITERS = 2
TILE_LAT = 4
TILE_LON = 16

TIME_STEP = 0.25
MEAN_DEPTH = 1.0
DRAG_RATE = 0.02
STEP_LENGTH = 0.3
CORIOLIS_MEAN = 0.3
CORIOLIS_SLOPE = 0.2
EPSILON = 1e-06

MESH = pl.DeviceIdType.MESH
LANES = 128
WIDTH = 1024
DIRECT_MAX = 64


def split3(x):
    hi = x.astype(jnp.bfloat16)
    rest = x - hi.astype(jnp.float32)
    mid = rest.astype(jnp.bfloat16)
    low = (rest - mid.astype(jnp.float32)).astype(jnp.bfloat16)
    return jnp.concatenate([hi, mid, low], axis=0)


def join3(y):
    n = y.shape[0] // 3
    return (y[2 * n :] + y[n : 2 * n]) + y[:n]


def fold_lanes(x):
    total = x[:, :LANES]
    for c in range(LANES, x.shape[1], LANES):
        total = total + x[:, c : c + LANES]
    return jnp.sum(total, axis=0, keepdims=True)


def kernel(
    n_tm, n_lat,
    states_hbm, background_hbm, error_hbm, mask_hbm, cells_hbm, moments_hbm, values_hbm, obs_err_hbm,
    est_out, slid_out, costs_out,
    xs, deriv, lam, forcing, onehot, gain, cor, masks, variance, inv_var,
    xnext, fe_prev, adj_in, dir_buf, dir_halo, dir_next, parts, parts_tm,
    error_std, land_mask, obs_cells, obs_moments, obs_values, obs_error,
    ssem, rsem, lsem,
):
    tm = lax.axis_index("tm")
    lat = lax.axis_index("lat")
    rows = variance.shape[1]
    lon = variance.shape[2]
    wide = 2 * rows
    half = STEPS
    width = min(WIDTH, lon)
    tiles = lon // width
    total_rows = rows * n_lat
    cell_count = 3 * total_rows * lon
    n_dev = n_tm * n_lat
    me = tm * n_lat + lat
    has_up = lat > 0
    has_down = lat < n_lat - 1
    has_prev = tm > 0
    has_next = tm < n_tm - 1
    up = {"lat": lat - 1}
    down = {"lat": lat + 1}
    before = {"tm": tm - 1}
    after = {"tm": tm + 1}
    direct = n_dev <= DIRECT_MAX

    def wrapped(i, n):
        return jnp.where(i >= n, i - n, i)

    lats = [lat] + [wrapped(lat + d, n_lat) for d in range(1, n_lat)]
    tms = [tm] + [wrapped(tm + d, n_tm) for d in range(1, n_tm)]
    lat_partners = [{"lat": lats[d]} for d in range(1, n_lat)]
    tm_partners = [{"tm": tms[d]} for d in range(1, n_tm)]
    if direct:
        all_partners = [
            {"tm": tms[t], "lat": lats[d]}
            for t in range(n_tm) for d in range(n_lat) if t or d
        ]
        partners = all_partners
    else:
        partners = lat_partners + tm_partners
    barrier = pltpu.get_barrier_semaphore()
    for partner in partners:
        pl.semaphore_signal(barrier, inc=1, device_id=partner, device_id_type=MESH)

    own = slice(0, rows)
    loads = []

    def load(src, dst):
        copy = pltpu.make_async_copy(src, dst, lsem.at[len(loads)])
        copy.start()
        loads.append(copy)

    load(states_hbm.at[0], xs.at[0, :, own])
    load(mask_hbm, land_mask)
    load(error_hbm, error_std)
    load(cells_hbm, obs_cells)
    load(moments_hbm, obs_moments)
    load(values_hbm, obs_values)
    load(obs_err_hbm, obs_error)
    for it in range(ITERS):
        @pl.when(tm == 0)
        def _(it=it):
            pltpu.make_async_copy(background_hbm, fe_prev.at[it], lsem.at[7 + it]).start()

    def remote(src, dst, k, device):
        return pltpu.make_async_remote_copy(
            src_ref=src, dst_ref=dst, send_sem=ssem.at[k], recv_sem=rsem.at[k],
            device_id=device, device_id_type=MESH,
        )

    pending = []
    late = []

    def send(cond, src, dst, k, device, queue=pending):
        @pl.when(cond)
        def _():
            remote(src, dst, k, device).start()

        queue.append((cond, src, k, device))

    def drain(queue):
        for cond, src, k, device in queue:
            @pl.when(cond)
            def _(src=src, k=k, device=device):
                remote(src, src, k, device).wait_send()
        queue.clear()

    def arrive(cond, dst, k, device):
        @pl.when(cond)
        def _():
            remote(dst, dst, k, device).wait_recv()

    zeros_half = jnp.zeros((3, half, lon), jnp.float32)
    lo, hi = slice(0, half), slice(half, rows)
    lo_w, hi_w = slice(rows, rows + half), slice(rows + half, wide)

    @pl.when(lat == n_lat - 1)
    def _():
        xs[0, :, lo_w, :] = zeros_half
        masks[lo_w, :] = jnp.zeros((half, LANES), jnp.float32)
        for it in range(ITERS):
            adj_in[it, :, hi, :] = zeros_half
            dir_halo[it, :, lo, :] = zeros_half

    @pl.when(lat == 0)
    def _():
        xs[0, :, hi_w, :] = zeros_half
        masks[hi_w, :] = jnp.zeros((half, LANES), jnp.float32)
        for it in range(ITERS):
            adj_in[it, :, lo, :] = zeros_half
            dir_halo[it, :, hi, :] = zeros_half

    @pl.when(tm == n_tm - 1)
    def _():
        xnext[...] = jnp.zeros(xnext.shape, jnp.float32)
        for it in range(ITERS):
            dir_next[it] = jnp.zeros(xnext.shape, jnp.float32)

    loads[1].wait()
    mask = land_mask[...].astype(jnp.float32)
    tile_cols = mask.shape[1]
    masks[own, :] = jnp.concatenate(
        [jnp.broadcast_to(mask[i : i + 1], (TILE_LAT, tile_cols)) for i in range(rows // TILE_LAT)],
        axis=0,
    )

    loads[0].wait()
    pl.semaphore_wait(barrier, len(partners))

    send(has_up, masks.at[lo], masks.at[lo_w], 0, up)
    send(has_down, masks.at[hi], masks.at[hi_w], 1, down)
    send(has_up, xs.at[0, :, lo], xs.at[0, :, lo_w], 2, up)
    send(has_down, xs.at[0, :, hi], xs.at[0, :, hi_w], 3, down)
    send(has_prev, xs.at[0, :, own], xnext, 4, before)

    for copy in loads[2:]:
        copy.wait()
    var = error_std[...] * error_std[...]
    variance[...] = var
    inv_var[...] = 1.0 / var
    cells = obs_cells[...]
    n_obs = cells.shape[1]
    cell_row = jnp.zeros_like(cells)
    for r in range(1, rows):
        cell_row = cell_row + (cells >= r * lon).astype(jnp.int32)
    cell_col = cells - cell_row * lon
    onehot[...] = (
        lax.broadcasted_iota(jnp.int32, (lon, n_obs), 0) == cell_col
    ).astype(jnp.float32).astype(jnp.bfloat16)
    taken = (
        lax.broadcasted_iota(jnp.int32, (STEPS * rows, n_obs), 0)
        == obs_moments[...] * rows + cell_row
    ).astype(jnp.float32)
    targets = obs_values[...]
    precision = 1.0 / (obs_error[...] * obs_error[...])
    r_id = lax.broadcasted_iota(jnp.int32, (wide, LANES), 0)
    r_id = jnp.where(r_id < rows + half, r_id, r_id - wide) + lat * rows
    cor[...] = CORIOLIS_MEAN + CORIOLIS_SLOPE * (r_id.astype(jnp.float32) / total_rows - 0.5)
    lam[STEPS, :, rows:wide, :] = jnp.zeros((3, rows, lon), jnp.float32)

    arrive(has_down, masks.at[lo_w], 0, down)
    arrive(has_up, masks.at[hi_w], 1, up)
    first_col = lax.broadcasted_iota(jnp.int32, (tile_cols, lon), 0) * TILE_LON
    col = lax.broadcasted_iota(jnp.int32, (tile_cols, lon), 1)
    grow = ((col >= first_col) & (col < first_col + TILE_LON)).astype(jnp.float32)
    gain[...] = TIME_STEP * jnp.dot(
        masks[...].astype(jnp.bfloat16), grow.astype(jnp.bfloat16),
        preferred_element_type=jnp.float32,
    )
    arrive(has_down, xs.at[0, :, lo_w], 2, down)
    arrive(has_up, xs.at[0, :, hi_w], 3, up)

    def ext(ref, index, j):
        c = j * width
        left = (c - LANES) % lon
        right = (c + width) % lon
        return jnp.concatenate(
            [
                ref[index + (slice(None), slice(left, left + LANES))],
                ref[index + (slice(None), slice(c, c + width))],
                ref[index + (slice(None), slice(right, right + LANES))],
            ],
            axis=-1,
        )

    def mid(e):
        return e[:, LANES : LANES + width]

    def dx2(e):
        return mid(pltpu.roll(e, width + 2 * LANES - 1, 1)) - mid(pltpu.roll(e, 1, 1))

    def east(e):
        return mid(pltpu.roll(e, width + 2 * LANES - 1, 1))

    def west(e):
        return mid(pltpu.roll(e, 1, 1))

    def north(a):
        return pltpu.roll(a, wide - 1, 0)

    def south(a):
        return pltpu.roll(a, 1, 0)

    def dy2(a):
        return north(a) - south(a)

    def coriolis():
        return jnp.concatenate([cor[...]] * (width // LANES), axis=-1)

    def forward_step(s, carry):
        for j in range(tiles):
            span = slice(j * width, (j + 1) * width)
            he, ue, ve = (ext(xs, (s, f), j) for f in range(3))
            h, u, v = mid(he), mid(ue), mid(ve)
            h_e, h_w, u_e, u_w = east(he), west(he), east(ue), west(ue)
            h_n, h_s, v_n, v_s = north(h), south(h), north(v), south(v)
            ux = 0.5 * (u_e - u_w)
            vx = 0.5 * dx2(ve)
            uy = 0.5 * dy2(u)
            vy = 0.5 * (v_n - v_s)
            g = gain[:, span]
            f = coriolis()
            dh = -0.5 * (
                ((MEAN_DEPTH + h_e) * u_e - (MEAN_DEPTH + h_w) * u_w)
                + ((MEAN_DEPTH + h_n) * v_n - (MEAN_DEPTH + h_s) * v_s)
            )
            du = f * v - 0.5 * (h_e - h_w) - u * ux - v * uy - DRAG_RATE * u
            dv = -f * u - 0.5 * (h_n - h_s) - u * vx - v * vy - DRAG_RATE * v
            xs[s + 1, 0, :, span] = h + g * dh
            xs[s + 1, 1, :, span] = u + g * du
            xs[s + 1, 2, :, span] = v + g * dv
            deriv[s, 0, :, span] = ux
            deriv[s, 1, :, span] = uy
            deriv[s, 2, :, span] = vx
            deriv[s, 3, :, span] = vy
        return carry

    def adjoint_step(i, carry):
        s = STEPS - 1 - i
        for j in range(tiles):
            span = slice(j * width, (j + 1) * width)
            ge = ext(gain, (), j)
            lh, lu, lv = (ext(lam, (s + 1, f), j) for f in range(3))
            ae, be, ce = lh * ge, lu * ge, lv * ge
            ue = ext(xs, (s, 1), j)
            a, b, c, u = mid(ae), mid(be), mid(ce), mid(ue)
            v = xs[s, 2, :, span]
            depth = 0.5 * (MEAN_DEPTH + xs[s, 0, :, span])
            f = coriolis()
            ax, ay = dx2(ae), dy2(a)
            obs = jnp.concatenate(
                [forcing[s, :, span], jnp.zeros((rows, width), jnp.float32)], axis=0
            )
            lam[s, 0, :, span] = (
                mid(lh) + obs + 0.5 * (u * ax + v * ay + dx2(be) + dy2(c))
            )
            lam[s, 1, :, span] = (
                mid(lu)
                + depth * ax
                + 0.5 * (dx2(ue * be) + dy2(v * b))
                - b * (deriv[s, 0, :, span] + DRAG_RATE)
                - c * (f + deriv[s, 2, :, span])
            )
            lam[s, 2, :, span] = (
                mid(lv)
                + depth * ay
                + 0.5 * (dx2(ue * ce) + dy2(v * c))
                + b * (f - deriv[s, 1, :, span])
                - c * (deriv[s, 3, :, span] + DRAG_RATE)
            )
        return carry

    def exchange(buf, value, k, size, mine, partner):
        buf[mine] = value
        for device in partner:
            remote(buf.at[mine], buf.at[mine], k, device).start()

    def collect(buf, k, size, partner):
        remote(buf.at[0 : size - 1], buf.at[0 : size - 1], k, partner[0]).wait_recv()
        total = jnp.sum(buf[...], axis=0)
        return total

    def sent(buf, k, size, partner):
        remote(buf.at[0 : size - 1], buf.at[0 : size - 1], k, partner[0]).wait_send()

    scale = None
    for it in range(ITERS):
        base = 5 + 8 * it
        lax.fori_loop(0, STEPS, forward_step, 0)
        send(has_next, xs.at[STEPS, :, own], fe_prev.at[it], base, after)

        heights = jnp.concatenate([xs[s, 0, own, :] for s in range(STEPS)], axis=0)
        seen = join3(
            jnp.dot(split3(heights), onehot[...], preferred_element_type=jnp.float32)
        )
        misfit = jnp.sum(seen * taken, axis=0, keepdims=True) - targets
        weighted = misfit * precision
        spread = join3(
            lax.dot_general(
                split3(taken * weighted), onehot[...], (((1,), (1,)), ((), ())),
                preferred_element_type=jnp.float32,
            )
        )
        for s in range(STEPS):
            forcing[s] = spread[s * rows : (s + 1) * rows]

        if it == 0:
            arrive(has_next, xnext, 4, after)
        else:
            arrive(has_next, dir_next.at[it - 1], base - 8 + 5, after)
            xnext[...] = xnext[...] - scale * dir_next[it - 1]

        @pl.when(has_next)
        def _():
            lam[STEPS, :, own, :] = (xs[STEPS, :, own, :] - xnext[...]) * inv_var[...]

        @pl.when(tm == n_tm - 1)
        def _():
            lam[STEPS, :, own, :] = jnp.zeros((3, rows, lon), jnp.float32)

        lax.fori_loop(0, STEPS, adjoint_step, 0)
        send(has_down, lam.at[0, :, lo_w], adj_in.at[it, :, lo], base + 1, down)
        send(has_up, lam.at[0, :, hi_w], adj_in.at[it, :, hi], base + 2, up)

        arrive(has_prev, fe_prev.at[it], base, before)

        @pl.when(tm == 0)
        def _():
            pltpu.make_async_copy(background_hbm, fe_prev.at[it], lsem.at[7 + it]).wait()

        cost = misfit * weighted
        for f in range(3):
            gap = xs[0, f, own, :] - fe_prev[it, f]
            cost = cost + fold_lanes(gap * gap * inv_var[f])
            dir_buf[it, f] = gap + variance[f] * lam[0, f, own, :]
        arrive(has_up, adj_in.at[it, :, lo], base + 1, up)
        arrive(has_down, adj_in.at[it, :, hi], base + 2, down)
        steep = jnp.zeros((1, LANES), jnp.float32)
        for f in range(3):
            direction = dir_buf[it, f] + variance[f] * adj_in[it, f]
            dir_buf[it, f] = direction
            steep = steep + fold_lanes(direction * direction * inv_var[f])

        message = jnp.concatenate([steep, cost], axis=0)
        if direct:
            exchange(parts.at[it], message, base + 6, n_dev, me, all_partners)
        else:
            exchange(parts.at[it], message, base + 6, n_lat, lat, lat_partners)
        send(has_up, dir_buf.at[it, :, lo], dir_halo.at[it, :, lo], base + 3, up, late)
        send(has_down, dir_buf.at[it, :, hi], dir_halo.at[it, :, hi], base + 4, down, late)
        drain(pending)
        if direct:
            send(has_prev, dir_buf.at[it], dir_next.at[it], base + 5, before, late)
            total = collect(parts.at[it], base + 6, n_dev, all_partners)
        else:
            total = collect(parts.at[it], base + 6, n_lat, lat_partners)
            exchange(parts_tm.at[it], total, base + 7, n_tm, tm, tm_partners)
            send(has_prev, dir_buf.at[it], dir_next.at[it], base + 5, before, late)
            total = collect(parts_tm.at[it], base + 7, n_tm, tm_partners)
        steepness = jnp.sum(total[0:1], axis=1, keepdims=True)
        scale = STEP_LENGTH / jnp.sqrt(steepness / (n_tm * cell_count) + EPSILON)
        costs_out[it] = jnp.sum(total[1:2]) * (0.5 / cell_count)

        for f in range(3):
            xs[0, f, own, :] = xs[0, f, own, :] - scale * dir_buf[it, f]
        arrive(has_down, dir_halo.at[it, :, lo], base + 3, down)
        arrive(has_up, dir_halo.at[it, :, hi], base + 4, up)
        for f in range(3):
            xs[0, f, rows:wide, :] = xs[0, f, rows:wide, :] - scale * dir_halo[it, f]

    est_copy = pltpu.make_async_copy(
        xs.at[0, :, own], est_out.at[0], lsem.at[7 + ITERS]
    )
    est_copy.start()
    lax.fori_loop(0, STEPS, forward_step, 0)
    arrive(has_next, dir_next.at[ITERS - 1], 5 + 8 * (ITERS - 1) + 5, after)

    @pl.when(has_next)
    def _():
        xnext[...] = xnext[...] - scale * dir_next[ITERS - 1]

    @pl.when(tm == n_tm - 1)
    def _():
        xnext[...] = xs[STEPS, :, own, :]

    slid_copy = pltpu.make_async_copy(xnext, slid_out.at[0], lsem.at[8 + ITERS])
    slid_copy.start()
    est_copy.wait()
    slid_copy.wait()
    drain(late)
    for it in range(ITERS):
        base = 5 + 8 * it
        if direct:
            sent(parts.at[it], base + 6, n_dev, all_partners)
        else:
            sent(parts.at[it], base + 6, n_lat, lat_partners)
            sent(parts_tm.at[it], base + 7, n_tm, tm_partners)


def write_out(est, slid, costs, est_out, slid_out, costs_out, est_v, slid_v, costs_s, sem):
    moves = []
    for i, (src, held) in enumerate(((est, est_v), (slid, slid_v), (costs, costs_s))):
        moves.append(pltpu.make_async_copy(src, held, sem.at[i]))
        moves[-1].start()
    outs = []
    for i, (held, dst) in enumerate(((est_v, est_out), (slid_v, slid_out), (costs_s, costs_out))):
        moves[i].wait()
        outs.append(pltpu.make_async_copy(held, dst, sem.at[3 + i]))
        outs[-1].start()
    for copy in outs:
        copy.wait()


def shards(n_tm, n_lat, *args):
    states, background = args[0], args[1]
    _, rows, lon = background.shape
    n_obs = args[4].shape[1]
    wide = 2 * rows
    f32 = jnp.float32
    direct = n_tm * n_lat <= DIRECT_MAX
    field = (3, rows, lon)
    sems = 5 + 8 * ITERS
    est, slid, costs = pl.pallas_call(
        functools.partial(kernel, n_tm, n_lat),
        out_shape=(
            jax.ShapeDtypeStruct(states.shape, f32),
            jax.ShapeDtypeStruct(states.shape, f32),
            jax.ShapeDtypeStruct((ITERS,), f32),
        ),
        in_specs=[pl.BlockSpec(memory_space=pltpu.HBM)] * 8,
        out_specs=(
            pl.BlockSpec(memory_space=pltpu.HBM),
            pl.BlockSpec(memory_space=pltpu.HBM),
            pl.BlockSpec(memory_space=pltpu.SMEM),
        ),
        scratch_shapes=[
            pltpu.VMEM((STEPS + 1, 3, wide, lon), f32),
            pltpu.VMEM((STEPS, 4, wide, lon), f32),
            pltpu.VMEM((STEPS + 1, 3, wide, lon), f32),
            pltpu.VMEM((STEPS, rows, lon), f32),
            pltpu.VMEM((lon, n_obs), jnp.bfloat16),
            pltpu.VMEM((wide, lon), f32),
            pltpu.VMEM((wide, LANES), f32),
            pltpu.VMEM((wide, LANES), f32),
            pltpu.VMEM(field, f32),
            pltpu.VMEM(field, f32),
            pltpu.VMEM(field, f32),
            pltpu.VMEM((ITERS,) + field, f32),
            pltpu.VMEM((ITERS,) + field, f32),
            pltpu.VMEM((ITERS,) + field, f32),
            pltpu.VMEM((ITERS,) + field, f32),
            pltpu.VMEM((ITERS,) + field, f32),
            pltpu.VMEM((ITERS, n_tm * n_lat if direct else n_lat, 2, LANES), f32),
            pltpu.VMEM((ITERS, n_tm, 2, LANES), f32),
            pltpu.VMEM(field, f32),
            pltpu.VMEM(args[3].shape, jnp.int32),
            pltpu.VMEM((1, n_obs), jnp.int32),
            pltpu.VMEM((1, n_obs), jnp.int32),
            pltpu.VMEM((1, n_obs), f32),
            pltpu.VMEM((1, n_obs), f32),
            pltpu.SemaphoreType.DMA((sems,)),
            pltpu.SemaphoreType.DMA((sems,)),
            pltpu.SemaphoreType.DMA((9 + ITERS,)),
        ],
        compiler_params=pltpu.CompilerParams(
            collective_id=0, has_side_effects=True
        ),
    )(*args)
    return pl.pallas_call(
        write_out,
        out_shape=(
            jax.ShapeDtypeStruct(states.shape, f32),
            jax.ShapeDtypeStruct(states.shape, f32),
            jax.ShapeDtypeStruct((ITERS,), f32),
        ),
        in_specs=[pl.BlockSpec(memory_space=pltpu.HBM)] * 3,
        out_specs=(pl.BlockSpec(memory_space=pltpu.HBM),) * 3,
        scratch_shapes=[
            pltpu.VMEM(states.shape, f32),
            pltpu.VMEM(states.shape, f32),
            pltpu.SMEM((ITERS,), f32),
            pltpu.SemaphoreType.DMA((6,)),
        ],
    )(est, slid, costs)


def solution(mesh):
    placed = (
        P("tm", None, "lat", None),
        P(None, "lat", None),
        P(None, "lat", None),
        P("lat", None),
        P("tm", "lat"),
        P("tm", "lat"),
        P("tm", "lat"),
        P("tm", "lat"),
    )
    return jax.shard_map(
        functools.partial(shards, mesh.shape["tm"], mesh.shape["lat"]),
        mesh=mesh,
        in_specs=placed,
        out_specs=(P("tm", None, "lat", None), P("tm", None, "lat", None), P()),
        check_vma=False,
    )
```
